32 devices in a mesh: sta: 8 (over y, x, core), win: 4 (over z).
Axes of the slice: x: 2, y: 2, z: 4, core: 2. Of those that a mesh axis runs over, the one named last changes fastest.
Arguments:
- green: bfloat16 [8, 3, 2, 256, 2048], P('sta', None, None, None, 'win'), may hold values from -0.0390625 to 0.0390625
- records: float32 [8, 3, 2, 2048], P('sta', None, None, 'win'), may hold values from -6 to 6
- onsets: int32 [256, 32], P('sta', 'win'), may hold values from 0 to 4095
- mask: int32 [8, 3], P('sta'), may hold values 0 or 1
Outputs:
- slip: float32 [256, 32], P('sta', 'win')
- direction: float32 [256, 32], P('sta', 'win')
- misfit: float32 [8, 3, 2, 2048], P('sta', None, None, 'win')
The draws below stay inside these ranges and needn't reach their ends.
All inputs are finite; a program needn't handle non-finite values. No bound on the sum of `mask` on one device may be relied on, other than what follows from the above.
Results may differ from the reference program's by a relative error of at most 0.007.
Values may be sent and summed in bfloat16 or wider, within the bound.
A program may use at most 64 MiB of HBM per device.

```python
import math
import jax
import jax.numpy as jnp
from jax import lax

COMP = 3
WINDOWS = 32
FREQS = 2048
SAMPLES = 4096
ITERS = 2
PATCHES = 256
STATIONS = 8


def with_ends(drawn, key, low, top_value):
    place = [jax.random.randint(jax.random.fold_in(key, axis), (), 0, length) for axis, length in enumerate(drawn.shape)]
    widest = drawn.shape.index(max(drawn.shape))
    beside = place[:widest] + [(place[widest] + 1) % drawn.shape[widest]] + place[widest + 1:]
    return drawn.at[tuple(place)].set(low).at[tuple(beside)].set(top_value)


def spiked(entries, key, source, target, blocks, factor):
    owner, partner = [(jnp.arange(entries.shape[position]) // (entries.shape[position] // blocks)).reshape([-1 if axis == position else 1 for axis in range(entries.ndim)]) for position in (source, target)]
    chosen = jax.random.permutation(key, blocks)[partner]
    strong = (owner == chosen) | (owner == (partner + blocks // 2) % blocks)
    return jnp.where(strong, factor * entries, entries)


def shard_levels(key, dims, split, low, high):
    gain, own = 1.0, jax.random.fold_in(key, 6)
    for position, blocks in split:
        heights = jnp.exp(jax.random.uniform(jax.random.fold_in(own, position), (blocks,), jnp.float32, low / len(split), high / len(split)))
        gain = gain * jnp.repeat(heights, dims[position] // blocks).reshape([-1 if axis == position else 1 for axis in range(len(dims))])
    return gain


def normal_values(rng, dims, deviation, limit, cuts=(), kind=jnp.bfloat16):
    result = deviation * jax.random.normal(rng, dims, jnp.float32)
    if cuts:
        result = result * shard_levels(rng, dims, cuts, -0.22, 0.18)
    return jnp.clip(result, -limit, limit).astype(kind)


def noise_with(key, shape, scale, most, shards, heavy, held_as=jnp.bfloat16):
    entries = scale * jax.random.normal(key, shape, jnp.float32)
    if shards:
        entries = entries * shard_levels(key, shape, shards, -0.22, 0.18)
    return jnp.clip(spiked(entries, jax.random.fold_in(key, 3), *heavy), -most, most).astype(held_as)


def setup_inputs(seed: int = 0) -> dict:
    key_of = jax.random.split(jax.random.key(seed), 5)
    green = noise_with(key_of[0], (STATIONS, COMP, 2, PATCHES, FREQS), (COMP * STATIONS * FREQS) ** -0.5, 0.0390625, ((0, 8), (4, 4)), (0, 3, 8, 2.0))
    records = normal_values(key_of[1], (STATIONS, COMP, 2, FREQS), 1.0, 6.0, ((0, 8), (3, 4)), jnp.float32)
    onsets = with_ends(jax.random.randint(key_of[2], (PATCHES, WINDOWS), 0, SAMPLES), jax.random.fold_in(key_of[2], 1), 0, SAMPLES - 1).astype(jnp.int32)
    mask = with_ends((jax.random.randint(key_of[3], (STATIONS, COMP), 0, 6) < 5).astype(jnp.int32), jax.random.fold_in(key_of[3], 1), 0, 1)
    return dict(green=green, records=records, onsets=onsets, mask=mask)


TWO_PI = 2.0 * math.pi

def phase_tables(onset_block, frequency):
    turns = onset_block[:, :, None] * frequency[None, None, :] % SAMPLES
    angle = turns.astype(jnp.float32) * (TWO_PI / SAMPLES)
    return (jnp.cos(angle), jnp.sin(angle))

def spectra_from(values, cosine, sine):
    real_part = lax.optimization_barrier(jnp.sum(values[:, :, None] * cosine, axis=1))
    imag_part = -lax.optimization_barrier(jnp.sum(values[:, :, None] * sine, axis=1))
    return jnp.stack([real_part, imag_part], axis=1).astype(jnp.bfloat16)

def project_with(combined, cosine, sine):
    return lax.optimization_barrier(jnp.sum(cosine * combined[:, 0, None, :] - sine * combined[:, 1, None, :], axis=2))

def spectra(model, onsets):
    frequency = jnp.arange(FREQS, dtype=jnp.int32)
    block = math.gcd(PATCHES, 256)

    def one_block(pair):
        values, onset_block = pair
        cosine, sine = phase_tables(onset_block, frequency)
        return spectra_from(values, cosine, sine)
    blocks = lax.map(one_block, (model.reshape(-1, block, WINDOWS), onsets.reshape(-1, block, WINDOWS)))
    return blocks.reshape(PATCHES, 2, FREQS)

def project(combined, onsets):
    frequency = jnp.arange(FREQS, dtype=jnp.int32)
    block = math.gcd(PATCHES, 256)

    def one_block(pair):
        parts, onset_block = pair
        cosine, sine = phase_tables(onset_block, frequency)
        return project_with(parts, cosine, sine)
    blocks = lax.map(one_block, (combined.reshape(-1, block, 2, FREQS), onsets.reshape(-1, block, WINDOWS)))
    return blocks.reshape(PATCHES, WINDOWS)

def forward(green, spectrum, weight):
    spec_re = spectrum[:, 0, :].astype(jnp.float32)
    spec_im = spectrum[:, 1, :].astype(jnp.float32)

    def one_station(station):
        green_re = station[:, 0].astype(jnp.float32)
        green_im = station[:, 1].astype(jnp.float32)
        real_part = lax.optimization_barrier(jnp.sum(green_re * spec_re - green_im * spec_im, axis=1))
        imag_part = lax.optimization_barrier(jnp.sum(green_re * spec_im + green_im * spec_re, axis=1))
        return jnp.stack([real_part, imag_part], axis=1)
    return lax.map(one_station, green) * weight

def adjoint(green, vector, weight, onsets):
    rounded = (vector * weight).astype(jnp.bfloat16)

    def add_station(total, item):
        station, trace = item
        green_re = station[:, 0].astype(jnp.float32)
        green_im = station[:, 1].astype(jnp.float32)
        trace_re = trace[:, 0].astype(jnp.float32)[:, None, :]
        trace_im = trace[:, 1].astype(jnp.float32)[:, None, :]
        part_re = lax.optimization_barrier(jnp.sum(green_re * trace_re + green_im * trace_im, axis=0))
        part_im = lax.optimization_barrier(jnp.sum(green_re * trace_im - green_im * trace_re, axis=0))
        return (total + jnp.stack([part_re, part_im], axis=1), None)
    start_total = jnp.zeros((PATCHES, 2, FREQS), jnp.float32)
    combined, unused = lax.scan(add_station, start_total, (green, rounded))
    return project(combined, onsets)

def reference(green, records, onsets, mask):
    weight = mask.astype(jnp.float32)[:, :, None, None]
    left = records * weight
    beta_norm = jnp.sqrt(jnp.sum(left * left))
    left = left / beta_norm
    right = adjoint(green, left, weight, onsets)
    alpha_norm = jnp.sqrt(jnp.sum(right * right))
    right = right / alpha_norm
    search = right
    estimate = jnp.zeros((PATCHES, WINDOWS), jnp.float32)
    phi_bar = beta_norm
    rho_bar = alpha_norm
    for sweep in range(ITERS):
        left = forward(green, spectra(right, onsets), weight) - alpha_norm * left
        beta_norm = jnp.sqrt(jnp.sum(left * left))
        left = left / beta_norm
        right = adjoint(green, left, weight, onsets) - beta_norm * right
        alpha_norm = jnp.sqrt(jnp.sum(right * right))
        right = right / alpha_norm
        rho_value = jnp.sqrt(rho_bar * rho_bar + beta_norm * beta_norm)
        cosine_rot = rho_bar / rho_value
        sine_rot = beta_norm / rho_value
        theta_rot = sine_rot * alpha_norm
        rho_bar = -cosine_rot * alpha_norm
        phi_step = cosine_rot * phi_bar
        phi_bar = sine_rot * phi_bar
        estimate = estimate + phi_step / rho_value * search
        search = right - theta_rot / rho_value * search
    return (estimate, search * math.sqrt(PATCHES * WINDOWS), phi_bar * left)
```

```python
import functools
import math

import jax
import jax.numpy as jnp
from jax import lax
from jax.experimental import pallas as pl
from jax.experimental.pallas import tpu as pltpu
from jax.sharding import PartitionSpec as P

SAMPLES = 4096
ITERS = 2
LANES = 128
ROWS = 16
GROUP = 4
MESH = pl.DeviceIdType.MESH


def cos_sin(turns):
    quarter = SAMPLES // 4
    shift = quarter.bit_length() - 1
    q = (turns + quarter // 2) >> shift
    x = (turns - (q << shift)).astype(jnp.float32) * (2.0 * math.pi / SAMPLES)
    y = x * x
    s = x + x * y * (-1 / 6 + y * (1 / 120 + y * (-1 / 5040 + y * (1 / 362880))))
    c = 1.0 + y * (-0.5 + y * (1 / 24 + y * (-1 / 720 + y * (1 / 40320))))
    odd = (q & 1) == 1
    cosine = jnp.where(odd, s, c)
    sine = jnp.where(odd, c, s)
    cosine = jnp.where(((q + 1) & 2) == 2, -cosine, cosine)
    sine = jnp.where((q & 2) == 2, -sine, sine)
    return cosine, sine


def kernel(cfg, green, rec, wrow, onset, est_out, dir_out, mis_out,
           on_recv, on_all, on_row, cos_t, sin_t, cd, cd_row, coef, qbuf, u, right, send, recv, piece, full,
           send_sem, recv_sem):
    nsta, nwin, patches, windows, bins, comps, local_w, local_p = cfg
    ndev = nsta * nwin
    nblk = bins // LANES
    npair = nblk // 2
    tiles = patches // LANES
    split = ndev // windows
    width = patches // split
    per_tile = LANES // local_p
    sta, win = lax.axis_index("sta"), lax.axis_index("win")
    me = sta * nwin + win

    def peer(k):
        other = lax.rem(me + k, ndev)
        return {"sta": other // nwin, "win": lax.rem(other, nwin)}, other

    barrier = pltpu.get_barrier_semaphore()

    def greet(k, carry):
        pl.semaphore_signal(barrier, inc=1, device_id=peer(k)[0], device_id_type=MESH)
        return carry

    lax.fori_loop(1, ndev, greet, 0)

    weight = wrow[...]

    def spread_of(src, dst, phase, indexed):
        def one(k, carry):
            where, other = peer(k)
            pltpu.make_async_remote_copy(
                src_ref=src.at[other] if indexed else src.at[0],
                dst_ref=dst.at[me],
                send_sem=send_sem.at[phase],
                recv_sem=recv_sem.at[phase],
                device_id=where,
                device_id_type=MESH,
            ).start()
            return carry
        lax.fori_loop(1, ndev, one, 0)
        pltpu.make_async_copy(src.at[me] if indexed else src.at[0], dst.at[me], recv_sem.at[phase]).start()

    def wait_all(dst, phase):
        pltpu.make_async_copy(dst, dst, recv_sem.at[phase]).wait()
        part = dst.at[pl.ds(0, ndev - 1)]
        pltpu.make_async_copy(part, part, send_sem.at[phase]).wait()

    def green_rows(comp, block, lo):
        rows = pl.ds(pl.multiple_of(block * LANES + lo, ROWS), ROWS)
        return (green[2 * comp, rows, :].astype(jnp.float32),
                green[2 * comp + 1, rows, :].astype(jnp.float32))

    def back_block(block, lo):
        rows = pl.ds(pl.multiple_of(block * LANES + lo, ROWS), ROWS)
        trace = u[rows, :] * weight
        re = im = None
        for comp in range(comps):
            gr, gi = green_rows(comp, block, lo)
            tr, ti = trace[:, 2 * comp:2 * comp + 1], trace[:, 2 * comp + 1:2 * comp + 2]
            a, b = gr * tr + gi * ti, gr * ti - gi * tr
            re, im = (a, b) if re is None else (re + a, im + b)
        return re, im

    def back_rows(lo):
        rows = pl.ds(lo, ROWS)
        for i in range(npair):
            ure, uim = back_block(npair + i, lo)
            lre, lim = back_block(npair - 1 - i, lo)
            qbuf[4 * i, rows, :] = ure + lre
            qbuf[4 * i + 1, rows, :] = uim + lim
            qbuf[4 * i + 2, rows, :] = ure - lre
            qbuf[4 * i + 3, rows, :] = uim - lim

    def project(norm2):
        def group(g, carry):
            for t in range(tiles):
                lanes = slice(t * LANES, (t + 1) * LANES)
                acc = [[None] * (2 * npair) for _ in range(GROUP)]
                for lb in range(LANES // 8):
                    rows = slice(lb * 8, lb * 8 + 8)
                    q = [qbuf[j, rows, lanes] for j in range(4 * npair)]
                    for j in range(GROUP):
                        c = cos_t[g * GROUP + j, rows, lanes]
                        s = sin_t[g * GROUP + j, rows, lanes]
                        for i in range(npair):
                            x = c * q[4 * i] - s * q[4 * i + 1]
                            y = c * q[4 * i + 3] + s * q[4 * i + 2]
                            if lb:
                                x, y = acc[j][2 * i] + x, acc[j][2 * i + 1] + y
                            acc[j][2 * i], acc[j][2 * i + 1] = x, y
                for j in range(GROUP):
                    w = g * GROUP + j
                    total = None
                    for i in range(npair):
                        part = (cd_row[2 * i, w, :, lanes] * acc[j][2 * i]
                                - cd_row[2 * i + 1, w, :, lanes] * acc[j][2 * i + 1])
                        total = part if total is None else total + part
                    row = jnp.sum(total, axis=0, keepdims=True)
                    at = t * LANES
                    send[w * split + at // width, :, at % width:at % width + LANES] = row
            return carry
        lax.fori_loop(0, windows // GROUP, group, 0)
        send[:, :, width:] = jnp.broadcast_to(norm2.reshape(1, 1, 1), (ndev, 1, LANES))

    def all_reduce(turn):
        spread_of(send, recv.at[turn], 1 + 2 * turn, True)
        wait_all(recv.at[turn], 1 + 2 * turn)
        summed = jnp.sum(recv[turn], axis=0)
        piece[0] = summed[:, :width]
        spread_of(piece, full.at[turn], 2 + 2 * turn, False)
        wait_all(full.at[turn], 2 + 2 * turn)
        return summed[:, width:width + 1]

    def image(turn):
        for d in range(ndev):
            at = d % split * width
            right[d // split:d // split + 1, at:at + width] = full[turn, d]
        return right[...]

    def square_sum(x):
        return jnp.sum(jnp.sum(x * x, axis=0, keepdims=True), axis=1, keepdims=True)

    u[...] = rec[...] * weight
    first_norm = square_sum(u[...])

    pl.semaphore_wait(barrier, ndev - 1)
    spread_of(onset, on_recv, 0, False)

    def first(step, carry):
        back_rows(pl.multiple_of(step * ROWS, ROWS))
        return carry
    lax.fori_loop(0, LANES // ROWS, first, 0)

    wait_all(on_recv, 0)
    for z in range(nwin):
        for t in range(tiles):
            block = on_recv[(t * per_tile) * nwin + z]
            for s in range(1, per_tile):
                block = block + on_recv[(t * per_tile + s) * nwin + z]
            on_all[z * local_w:(z + 1) * local_w, t * LANES:(t + 1) * LANES] = block
    for i in range(npair):
        c, s = cos_sin(on_all[...] * (LANES // 2 + i * LANES))
        cd[2 * i], cd[2 * i + 1] = c, s
        for w in range(windows):
            cd_row[2 * i, w], cd_row[2 * i + 1, w] = c[w:w + 1], s[w:w + 1]
    for w in range(windows):
        on_row[w] = on_all[w:w + 1, :]
    centre = win * bins + (bins - LANES) // 2

    def tables(w, carry):
        rowv = on_row[w]
        for lb in range(LANES // ROWS):
            freq = lax.broadcasted_iota(jnp.int32, (ROWS, patches), 0) + (centre + lb * ROWS)
            c, s = cos_sin(freq * rowv)
            cos_t[w, lb * ROWS:(lb + 1) * ROWS, :] = c
            sin_t[w, lb * ROWS:(lb + 1) * ROWS, :] = s
        return carry
    lax.fori_loop(0, windows, tables, 0)

    project(first_norm)
    norm2 = all_reduce(0)
    beta = jnp.sqrt(norm2)
    v = image(0) / beta
    alpha = jnp.sqrt(square_sum(v))
    v = v / alpha
    search = v
    estimate = jnp.zeros_like(v)
    phi_bar, rho_bar = beta, alpha

    for sweep in range(ITERS):
        for i in range(npair):
            coef[2 * i] = v * cd[2 * i]
            coef[2 * i + 1] = v * cd[2 * i + 1]
        right[...] = v

        def forward(step, carry, alpha=alpha, beta=beta):
            lo = pl.multiple_of(step * ROWS, ROWS)
            spectra = [[] for _ in range(2 * nblk)]
            for t in range(tiles):
                lanes = slice(t * LANES, (t + 1) * LANES)
                acc = None
                for w in range(windows):
                    c = cos_t[w, pl.ds(lo, ROWS), lanes]
                    s = sin_t[w, pl.ds(lo, ROWS), lanes]
                    terms = []
                    for i in range(2 * npair):
                        a = coef[i, w:w + 1, lanes]
                        terms += [a * c, a * s]
                    acc = terms if acc is None else [x + y for x, y in zip(acc, terms)]
                for i in range(npair):
                    x1, x2, y1, y2 = acc[4 * i:4 * i + 4]
                    up, low = npair + i, npair - 1 - i
                    spectra[2 * up].append(x1 - y2)
                    spectra[2 * up + 1].append(-x2 - y1)
                    spectra[2 * low].append(x1 + y2)
                    spectra[2 * low + 1].append(y1 - x2)
            lane = lax.broadcasted_iota(jnp.int32, (ROWS, LANES), 1)
            for block in range(nblk):
                sre, sim = [[x.astype(jnp.bfloat16).astype(jnp.float32) for x in spectra[2 * block + k]] for k in range(2)]
                data = jnp.zeros((ROWS, LANES), jnp.float32)
                for comp in range(comps):
                    gr, gi = green_rows(comp, block, lo)
                    re = im = 0.0
                    for t in range(tiles):
                        lanes = slice(t * LANES, (t + 1) * LANES)
                        re = re + (gr[:, lanes] * sre[t] - gi[:, lanes] * sim[t])
                        im = im + (gr[:, lanes] * sim[t] + gi[:, lanes] * sre[t])
                    data = jnp.where(lane == 2 * comp, jnp.sum(re, axis=1, keepdims=True), data)
                    data = jnp.where(lane == 2 * comp + 1, jnp.sum(im, axis=1, keepdims=True), data)
                rows = pl.ds(pl.multiple_of(block * LANES + lo, ROWS), ROWS)
                u[rows, :] = data * weight - (alpha / beta) * u[rows, :]
            back_rows(lo)
            return carry
        lax.fori_loop(0, LANES // ROWS, forward, 0)

        project(square_sum(u[...]))
        norm2 = all_reduce(1 + sweep)
        old = right[...]
        beta = jnp.sqrt(norm2)
        v = image(1 + sweep) / beta - beta * old
        alpha = jnp.sqrt(square_sum(v))
        v = v / alpha
        rho = jnp.sqrt(rho_bar * rho_bar + beta * beta)
        cosine_rot = rho_bar / rho
        sine_rot = beta / rho
        theta = sine_rot * alpha
        rho_bar = -cosine_rot * alpha
        phi = cosine_rot * phi_bar
        phi_bar = sine_rot * phi_bar
        estimate = estimate + phi / rho * search
        search = v - theta / rho * search
    est_out[...] = estimate
    dir_out[...] = search * math.sqrt(patches * windows)
    mis_out[...] = (phi_bar / beta) * u[...]


def local(nsta, nwin, green, records, onsets, mask):
    local_p, local_w = onsets.shape
    comps = green.shape[1]
    patches, windows = local_p * nsta, local_w * nwin
    bins = green.shape[4]
    ndev = nsta * nwin
    width = patches * windows // ndev
    npair = bins // LANES // 2
    columns = 2 * comps
    green_t = jnp.swapaxes(green.reshape(columns, patches, bins), 1, 2)
    rec = jnp.pad(records.reshape(columns, bins).T, ((0, 0), (0, LANES - columns)))
    weight = jnp.pad(jnp.repeat(mask.astype(jnp.float32), 2, axis=1), ((0, 0), (0, LANES - columns)))
    sta, win = lax.axis_index("sta"), lax.axis_index("win")
    group = LANES // local_p
    mine = jnp.arange(LANES) // local_p == sta % group
    onset = jnp.where(mine[None, :], jnp.tile(onsets.T, (1, group)), 0)[None]
    cfg = (nsta, nwin, patches, windows, bins, comps, local_w, local_p)
    f32 = jnp.float32
    turns = ITERS + 1
    est, direction, misfit = pl.pallas_call(
        functools.partial(kernel, cfg),
        out_shape=(jax.ShapeDtypeStruct((windows, patches), f32),
                   jax.ShapeDtypeStruct((windows, patches), f32),
                   jax.ShapeDtypeStruct((bins, LANES), f32)),
        in_specs=[pl.BlockSpec(memory_space=pltpu.VMEM)] * 4,
        out_specs=(pl.BlockSpec(memory_space=pltpu.VMEM),) * 3,
        scratch_shapes=[
            pltpu.VMEM((ndev, local_w, LANES), jnp.int32),
            pltpu.VMEM((windows, patches), jnp.int32),
            pltpu.VMEM((windows, 1, patches), jnp.int32),
            pltpu.VMEM((windows, LANES, patches), f32),
            pltpu.VMEM((windows, LANES, patches), f32),
            pltpu.VMEM((2 * npair, windows, patches), f32),
            pltpu.VMEM((2 * npair, windows, 1, patches), f32),
            pltpu.VMEM((2 * npair, windows, patches), f32),
            pltpu.VMEM((4 * npair, LANES, patches), f32),
            pltpu.VMEM((bins, LANES), f32),
            pltpu.VMEM((windows, patches), f32),
            pltpu.VMEM((ndev, 1, width + LANES), f32),
            pltpu.VMEM((turns, ndev, 1, width + LANES), f32),
            pltpu.VMEM((1, 1, width), f32),
            pltpu.VMEM((turns, ndev, 1, width), f32),
            pltpu.SemaphoreType.DMA((1 + 2 * turns,)),
            pltpu.SemaphoreType.DMA((1 + 2 * turns,)),
        ],
        compiler_params=pltpu.CompilerParams(
            collective_id=0, has_side_effects=True, vmem_limit_bytes=56 * 2**20),
    )(green_t, rec, weight, onset)
    def mine_of(x):
        return lax.dynamic_slice(x, (win * local_w, sta * local_p), (local_w, local_p)).T
    left = misfit[:, :columns].T.reshape(1, comps, 2, bins)
    return mine_of(est), mine_of(direction), left


def solution(mesh):
    return jax.shard_map(
        functools.partial(local, mesh.shape["sta"], mesh.shape["win"]),
        mesh=mesh,
        in_specs=(
            P("sta", None, None, None, "win"),
            P("sta", None, None, "win"),
            P("sta", "win"),
            P("sta", None),
        ),
        out_specs=(P("sta", "win"), P("sta", "win"), P("sta", None, None, "win")),
        check_vma=False,
    )
```

```python
import functools
import math

import jax
import jax.numpy as jnp
from jax import lax
from jax.experimental import pallas as pl
from jax.experimental.pallas import tpu as pltpu
from jax.sharding import PartitionSpec as P

SAMPLES = 4096
ITERS = 2
LANES = 128
ROWS = 16
GROUP = 4
MESH = pl.DeviceIdType.MESH


def cos_sin(turns):
    quarter = SAMPLES // 4
    shift = quarter.bit_length() - 1
    q = (turns + quarter // 2) >> shift
    x = (turns - (q << shift)).astype(jnp.float32) * (2.0 * math.pi / SAMPLES)
    y = x * x
    s = x + x * y * (-1 / 6 + y * (1 / 120 + y * (-1 / 5040 + y * (1 / 362880))))
    c = 1.0 + y * (-0.5 + y * (1 / 24 + y * (-1 / 720 + y * (1 / 40320))))
    odd = (q & 1) == 1
    cosine = jnp.where(odd, s, c)
    sine = jnp.where(odd, c, s)
    cosine = jnp.where(((q + 1) & 2) == 2, -cosine, cosine)
    sine = jnp.where((q & 2) == 2, -sine, sine)
    return cosine, sine


def kernel(cfg, green_in, rec, onset_in, mask, est_out, dir_out, mis_out,
           green_raw, green, green_sem, tmp, onset, on_recv, on_all, on_row, cos_t, sin_t, cd, cd_row, coef, qbuf, u, right, turned, send, recv, piece, full,
           send_sem, recv_sem):
    nsta, nwin, patches, windows, bins, comps, local_w, local_p = cfg
    ndev = nsta * nwin
    nblk = bins // LANES
    npair = nblk // 2
    tiles = patches // LANES
    split = ndev // windows
    width = patches // split
    per_tile = LANES // local_p
    sta, win = lax.axis_index("sta"), lax.axis_index("win")
    me = sta * nwin + win

    def wrapped(x, size):
        return jnp.where(x >= size, x - size, x)

    stas = [wrapped(sta + k, nsta) for k in range(nsta)]
    wins = [wrapped(win + k, nwin) for k in range(nwin)]
    near = sorted(range(nwin), key=lambda k: -min(k, nwin - k))
    peers = [(stas[a], wins[b]) for b in near for a in range(nsta - 1, -1, -1) if a or b]

    barrier = pltpu.get_barrier_semaphore()
    for other_sta, other_win in peers:
        pl.semaphore_signal(barrier, inc=1, device_id={"sta": other_sta, "win": other_win},
                            device_id_type=MESH)
    green_copy = pltpu.make_async_copy(green_in, green_raw, green_sem)
    green_copy.start()

    lane_row = lax.broadcasted_iota(jnp.int32, (1, LANES), 1)
    weight = jnp.zeros((1, LANES), jnp.float32)
    for comp in range(comps):
        on = jnp.full((1, LANES), mask[0, comp], jnp.int32).astype(jnp.float32)
        weight = jnp.where(lane_row // 2 == comp, on, weight)

    def remote(src, dst, phase, other_sta, other_win):
        return pltpu.make_async_remote_copy(
            src_ref=src, dst_ref=dst, send_sem=send_sem.at[phase], recv_sem=recv_sem.at[phase],
            device_id={"sta": other_sta, "win": other_win}, device_id_type=MESH)

    def spread(src, dst, phase):
        for other_sta, other_win in peers:
            remote(src.at[0], dst.at[me], phase, other_sta, other_win).start()
        pltpu.make_async_copy(src.at[0], dst.at[me], recv_sem.at[phase]).start()

    def wait_all(dst, phase):
        pltpu.make_async_copy(dst, dst, recv_sem.at[phase]).wait()
        part = dst.at[pl.ds(0, ndev - 1)]
        pltpu.make_async_copy(part, part, send_sem.at[phase]).wait()

    def green_rows(comp, block, lo):
        rows = pl.ds(pl.multiple_of(block * LANES + lo, ROWS), ROWS)
        return (green[2 * comp, rows, :].astype(jnp.float32),
                green[2 * comp + 1, rows, :].astype(jnp.float32))

    def back_block(block, lo):
        rows = pl.ds(pl.multiple_of(block * LANES + lo, ROWS), ROWS)
        trace = u[rows, :] * weight
        re = im = None
        for comp in range(comps):
            gr, gi = green_rows(comp, block, lo)
            tr, ti = trace[:, 2 * comp:2 * comp + 1], trace[:, 2 * comp + 1:2 * comp + 2]
            a, b = gr * tr + gi * ti, gr * ti - gi * tr
            re, im = (a, b) if re is None else (re + a, im + b)
        return re, im

    def back_rows(lo):
        rows = pl.ds(lo, ROWS)
        for i in range(npair):
            ure, uim = back_block(npair + i, lo)
            lre, lim = back_block(npair - 1 - i, lo)
            qbuf[4 * i, rows, :] = ure + lre
            qbuf[4 * i + 1, rows, :] = uim + lim
            qbuf[4 * i + 2, rows, :] = ure - lre
            qbuf[4 * i + 3, rows, :] = uim - lim

    def project(norm2, turn):
        norm_row = jnp.broadcast_to(norm2, (1, LANES))

        def group(g, carry):
            for t in range(tiles):
                lanes = slice(t * LANES, (t + 1) * LANES)
                acc = [[None] * (2 * npair) for _ in range(GROUP)]
                for lb in range(LANES // 8):
                    rows = slice(lb * 8, lb * 8 + 8)
                    q = [qbuf[j, rows, lanes] for j in range(4 * npair)]
                    for j in range(GROUP):
                        c = cos_t[g * GROUP + j, rows, lanes]
                        s = sin_t[g * GROUP + j, rows, lanes]
                        for i in range(npair):
                            x = c * q[4 * i] - s * q[4 * i + 1]
                            y = c * q[4 * i + 3] + s * q[4 * i + 2]
                            if lb:
                                x, y = acc[j][2 * i] + x, acc[j][2 * i + 1] + y
                            acc[j][2 * i], acc[j][2 * i + 1] = x, y
                for j in range(GROUP):
                    w = g * GROUP + j
                    total = None
                    for i in range(npair):
                        part = (cd_row[2 * i, w, :, lanes] * acc[j][2 * i]
                                - cd_row[2 * i + 1, w, :, lanes] * acc[j][2 * i + 1])
                        total = part if total is None else total + part
                    row = jnp.sum(total, axis=0, keepdims=True)
                    at = t * LANES
                    send[w * split + at // width, :, at % width:at % width + LANES] = row
            for j in range(GROUP * split):
                d = g * (GROUP * split) + j
                send[d, :, width:] = norm_row
                phase = 1 + 2 * turn

                @pl.when(d != me)
                def _():
                    remote(send.at[d], recv.at[turn, me], phase, d // nwin, lax.rem(d, nwin)).start()

                @pl.when(d == me)
                def _():
                    pltpu.make_async_copy(send.at[d], recv.at[turn, me], recv_sem.at[phase]).start()
            return carry
        lax.fori_loop(0, windows // GROUP, group, 0)

    def all_reduce(turn):
        wait_all(recv.at[turn], 1 + 2 * turn)
        summed = jnp.sum(recv[turn], axis=0)
        piece[0] = summed[:, :width]
        spread(piece, full.at[turn], 2 + 2 * turn)
        wait_all(full.at[turn], 2 + 2 * turn)
        return summed[:, width:width + 1]

    def image(turn):
        for d in range(ndev):
            at = d % split * width
            right[d // split:d // split + 1, at:at + width] = full[turn, d]
        return right[...]

    def square_sum(x):
        return jnp.sum(jnp.sum(x * x, axis=0, keepdims=True), axis=1, keepdims=True)

    tmp[:, 0:LANES] = jnp.zeros((LANES, LANES), jnp.float32)
    start = pl.multiple_of(lax.rem(sta, per_tile) * local_p, local_p)
    tmp[pl.ds(start, local_p), 0:local_w] = onset_in[...].astype(jnp.float32)
    onset[0] = tmp[:, 0:LANES].T[0:local_w, :]
    pl.semaphore_wait(barrier, ndev - 1)
    spread(onset, on_recv, 0)

    tmp[...] = jnp.zeros_like(tmp)
    for comp in range(comps):
        for part in range(2):
            tmp[2 * comp + part:2 * comp + part + 1, 0:bins] = rec[0, comp, part:part + 1, :]
    for block in range(nblk):
        lanes = slice(block * LANES, (block + 1) * LANES)
        u[lanes, :] = tmp[:, lanes].T * weight
    first_norm = square_sum(u[...])
    green_copy.wait()
    for comp in range(comps):
        for part in range(2):
            for block in range(nblk):
                rows = slice(block * LANES, (block + 1) * LANES)
                for t in range(tiles):
                    lanes = slice(t * LANES, (t + 1) * LANES)
                    green[2 * comp + part, rows, lanes] = green_raw[0, comp, part, lanes, rows].T

    def first(step, carry):
        back_rows(pl.multiple_of(step * ROWS, ROWS))
        return carry
    lax.fori_loop(0, LANES // ROWS, first, 0)

    wait_all(on_recv, 0)
    for z in range(nwin):
        for t in range(tiles):
            block = on_recv[(t * per_tile) * nwin + z]
            for s in range(1, per_tile):
                block = block + on_recv[(t * per_tile + s) * nwin + z]
            on_all[z * local_w:(z + 1) * local_w, t * LANES:(t + 1) * LANES] = block.astype(jnp.int32)
    for i in range(npair):
        c, s = cos_sin(on_all[...] * (LANES // 2 + i * LANES))
        cd[2 * i], cd[2 * i + 1] = c, s
        for w in range(windows):
            cd_row[2 * i, w], cd_row[2 * i + 1, w] = c[w:w + 1], s[w:w + 1]
    for w in range(windows):
        on_row[w] = on_all[w:w + 1, :]
    centre = win * bins + (bins - LANES) // 2

    def tables(w, carry):
        rowv = on_row[w]
        low = lax.broadcasted_iota(jnp.int32, (ROWS, patches), 0) + centre
        c0, s0 = cos_sin(low * rowv)
        high = lax.broadcasted_iota(jnp.int32, (LANES // ROWS, patches), 0) * ROWS
        c1, s1 = cos_sin(high * rowv)
        cos_t[w, 0:ROWS, :] = c0
        sin_t[w, 0:ROWS, :] = s0
        for lb in range(1, LANES // ROWS):
            ch, sh = c1[lb:lb + 1], s1[lb:lb + 1]
            cos_t[w, lb * ROWS:(lb + 1) * ROWS, :] = c0 * ch - s0 * sh
            sin_t[w, lb * ROWS:(lb + 1) * ROWS, :] = s0 * ch + c0 * sh
        return carry
    lax.fori_loop(0, windows, tables, 0)

    project(first_norm, 0)
    norm2 = all_reduce(0)
    beta = jnp.sqrt(norm2)
    v = image(0) / beta
    alpha = jnp.sqrt(square_sum(v))
    v = v / alpha
    search = v
    estimate = jnp.zeros_like(v)
    phi_bar, rho_bar = beta, alpha

    for sweep in range(ITERS):
        for i in range(npair):
            coef[2 * i] = v * cd[2 * i]
            coef[2 * i + 1] = v * cd[2 * i + 1]
        right[...] = v

        def forward(step, carry, alpha=alpha, beta=beta):
            lo = pl.multiple_of(step * ROWS, ROWS)
            spectra = [[] for _ in range(2 * nblk)]
            for t in range(tiles):
                lanes = slice(t * LANES, (t + 1) * LANES)
                acc = None
                for w in range(windows):
                    c = cos_t[w, pl.ds(lo, ROWS), lanes]
                    s = sin_t[w, pl.ds(lo, ROWS), lanes]
                    terms = []
                    for i in range(2 * npair):
                        a = coef[i, w:w + 1, lanes]
                        terms += [a * c, a * s]
                    acc = terms if acc is None else [x + y for x, y in zip(acc, terms)]
                for i in range(npair):
                    x1, x2, y1, y2 = acc[4 * i:4 * i + 4]
                    up, low = npair + i, npair - 1 - i
                    spectra[2 * up].append(x1 - y2)
                    spectra[2 * up + 1].append(-x2 - y1)
                    spectra[2 * low].append(x1 + y2)
                    spectra[2 * low + 1].append(y1 - x2)
            lane = lax.broadcasted_iota(jnp.int32, (ROWS, LANES), 1)
            for block in range(nblk):
                sre, sim = [[x.astype(jnp.bfloat16).astype(jnp.float32) for x in spectra[2 * block + k]] for k in range(2)]
                data = jnp.zeros((ROWS, LANES), jnp.float32)
                for comp in range(comps):
                    gr, gi = green_rows(comp, block, lo)
                    re = im = 0.0
                    for t in range(tiles):
                        lanes = slice(t * LANES, (t + 1) * LANES)
                        re = re + (gr[:, lanes] * sre[t] - gi[:, lanes] * sim[t])
                        im = im + (gr[:, lanes] * sim[t] + gi[:, lanes] * sre[t])
                    data = jnp.where(lane == 2 * comp, jnp.sum(re, axis=1, keepdims=True), data)
                    data = jnp.where(lane == 2 * comp + 1, jnp.sum(im, axis=1, keepdims=True), data)
                rows = pl.ds(pl.multiple_of(block * LANES + lo, ROWS), ROWS)
                u[rows, :] = data * weight - (alpha / beta) * u[rows, :]
            back_rows(lo)
            return carry
        lax.fori_loop(0, LANES // ROWS, forward, 0)

        project(square_sum(u[...]), 1 + sweep)
        norm2 = all_reduce(1 + sweep)
        old = right[...]
        beta = jnp.sqrt(norm2)
        v = image(1 + sweep) / beta - beta * old
        alpha = jnp.sqrt(square_sum(v))
        v = v / alpha
        rho = jnp.sqrt(rho_bar * rho_bar + beta * beta)
        cosine_rot = rho_bar / rho
        sine_rot = beta / rho
        theta = sine_rot * alpha
        rho_bar = -cosine_rot * alpha
        phi = cosine_rot * phi_bar
        phi_bar = sine_rot * phi_bar
        estimate = estimate + phi / rho * search
        search = v - theta / rho * search
    tmp[...] = jnp.zeros_like(tmp)
    for value, out in ((estimate, est_out), (search * math.sqrt(patches * windows), dir_out)):
        tmp[0:windows, 0:patches] = value
        for t in range(tiles):
            lanes = slice(t * LANES, (t + 1) * LANES)
            turned[lanes, :] = tmp[:, lanes].T
        rows = turned[pl.ds(pl.multiple_of(sta * local_p, local_p), local_p), :]
        own = rows[:, 0:local_w]
        for z in range(1, nwin):
            own = jnp.where(win == z, rows[:, z * local_w:(z + 1) * local_w], own)
        out[...] = own
    scale = phi_bar / beta
    for block in range(nblk):
        lanes = slice(block * LANES, (block + 1) * LANES)
        flipped = (u[lanes, :] * scale).T
        for comp in range(comps):
            mis_out[0, comp, :, lanes] = flipped[2 * comp:2 * comp + 2, :]


def local(nsta, nwin, green, records, onsets, mask):
    local_p, local_w = onsets.shape
    comps = green.shape[1]
    patches, windows = local_p * nsta, local_w * nwin
    bins = green.shape[4]
    ndev = nsta * nwin
    width = patches * windows // ndev
    npair = bins // LANES // 2
    cfg = (nsta, nwin, patches, windows, bins, comps, local_w, local_p)
    f32 = jnp.float32
    turns = ITERS + 1
    return pl.pallas_call(
        functools.partial(kernel, cfg),
        out_shape=(jax.ShapeDtypeStruct((local_p, local_w), f32),
                   jax.ShapeDtypeStruct((local_p, local_w), f32),
                   jax.ShapeDtypeStruct((1, comps, 2, bins), f32)),
        in_specs=[pl.BlockSpec(memory_space=pl.ANY),
                  pl.BlockSpec(memory_space=pltpu.VMEM),
                  pl.BlockSpec(memory_space=pltpu.VMEM),
                  pl.BlockSpec(memory_space=pltpu.SMEM)],
        out_specs=(pl.BlockSpec(memory_space=pltpu.VMEM),) * 3,
        scratch_shapes=[
            pltpu.VMEM((1, comps, 2, patches, bins), jnp.bfloat16),
            pltpu.VMEM((2 * comps, bins, patches), jnp.bfloat16),
            pltpu.SemaphoreType.DMA,
            pltpu.VMEM((LANES, max(bins, patches)), f32),
            pltpu.VMEM((1, local_w, LANES), f32),
            pltpu.VMEM((ndev, local_w, LANES), f32),
            pltpu.VMEM((windows, patches), jnp.int32),
            pltpu.VMEM((windows, 1, patches), jnp.int32),
            pltpu.VMEM((windows, LANES, patches), f32),
            pltpu.VMEM((windows, LANES, patches), f32),
            pltpu.VMEM((2 * npair, windows, patches), f32),
            pltpu.VMEM((2 * npair, windows, 1, patches), f32),
            pltpu.VMEM((2 * npair, windows, patches), f32),
            pltpu.VMEM((4 * npair, LANES, patches), f32),
            pltpu.VMEM((bins, LANES), f32),
            pltpu.VMEM((windows, patches), f32),
            pltpu.VMEM((patches, LANES), f32),
            pltpu.VMEM((ndev, 1, width + LANES), f32),
            pltpu.VMEM((turns, ndev, 1, width + LANES), f32),
            pltpu.VMEM((1, 1, width), f32),
            pltpu.VMEM((turns, ndev, 1, width), f32),
            pltpu.SemaphoreType.DMA((1 + 2 * turns,)),
            pltpu.SemaphoreType.DMA((1 + 2 * turns,)),
        ],
        compiler_params=pltpu.CompilerParams(
            collective_id=0, has_side_effects=True, vmem_limit_bytes=56 * 2**20),
    )(green, records, onsets, mask)


def solution(mesh):
    return jax.shard_map(
        functools.partial(local, mesh.shape["sta"], mesh.shape["win"]),
        mesh=mesh,
        in_specs=(
            P("sta", None, None, None, "win"),
            P("sta", None, None, "win"),
            P("sta", "win"),
            P("sta", None),
        ),
        out_specs=(P("sta", "win"), P("sta", "win"), P("sta", None, None, "win")),
        check_vma=False,
    )
```

```python
import functools
import math

import jax
import jax.numpy as jnp
from jax import lax
from jax.experimental import pallas as pl
from jax.experimental.pallas import tpu as pltpu
from jax.sharding import PartitionSpec as P

SAMPLES = 4096
ITERS = 2
LANES = 128
ROWS = 16
MESH = pl.DeviceIdType.MESH


def cos_sin(turns):
    quarter = SAMPLES // 4
    shift = quarter.bit_length() - 1
    q = (turns + quarter // 2) >> shift
    x = (turns - (q << shift)).astype(jnp.float32) * (2.0 * math.pi / SAMPLES)
    y = x * x
    s = x + x * y * (-1 / 6 + y * (1 / 120 + y * (-1 / 5040 + y * (1 / 362880))))
    c = 1.0 + y * (-0.5 + y * (1 / 24 + y * (-1 / 720 + y * (1 / 40320))))
    odd = (q & 1) == 1
    cosine = jnp.where(odd, s, c)
    sine = jnp.where(odd, c, s)
    cosine = jnp.where(((q + 1) & 2) == 2, -cosine, cosine)
    sine = jnp.where((q & 2) == 2, -sine, sine)
    return cosine, sine


def kernel(cfg, green_in, rec_in, onset_in, mask, est_out, dir_out, mis_out,
           green_raw, green, green_sem, rec, rec_sem, onset_own, onset_sem, tmp, onset, on_recv, on_all, on_row, cos_t, sin_t, cd, cd_row, coef, qbuf, u, right, turned, send, recv, piece, level, total_piece, full,
           send_sem, recv_sem):
    nsta, nwin, patches, windows, bins, comps, local_w, local_p = cfg
    ndev = nsta * nwin
    nblk = bins // LANES
    npair = nblk // 2
    tiles = patches // LANES
    group_rows = windows // nsta
    width = patches
    per_tile = LANES // local_p
    sta, win = lax.axis_index("sta"), lax.axis_index("win")
    me = sta * nwin + win

    def wrapped(x, size):
        return jnp.where(x >= size, x - size, x)

    stas = [wrapped(sta + k, nsta) for k in range(nsta)]
    wins = [wrapped(win + k, nwin) for k in range(nwin)]
    near = sorted(range(nwin), key=lambda k: -min(k, nwin - k))
    peers = [(stas[a], wins[b]) for b in near for a in range(nsta - 1, -1, -1) if a or b]

    barrier = pltpu.get_barrier_semaphore()
    for other_sta, other_win in peers:
        pl.semaphore_signal(barrier, inc=1, device_id={"sta": other_sta, "win": other_win},
                            device_id_type=MESH)
    onset_copy = pltpu.make_async_copy(onset_in, onset_own, onset_sem)
    onset_copy.start()
    rec_copy = pltpu.make_async_copy(rec_in, rec, rec_sem)
    rec_copy.start()
    green_copy = pltpu.make_async_copy(green_in, green_raw, green_sem)
    green_copy.start()

    lane_row = lax.broadcasted_iota(jnp.int32, (1, LANES), 1)
    weight = jnp.zeros((1, LANES), jnp.float32)
    for comp in range(comps):
        on = jnp.full((1, LANES), mask[0, comp], jnp.int32).astype(jnp.float32)
        weight = jnp.where(lane_row // 2 == comp, on, weight)

    def remote(src, dst, phase, other_sta, other_win):
        return pltpu.make_async_remote_copy(
            src_ref=src, dst_ref=dst, send_sem=send_sem.at[phase], recv_sem=recv_sem.at[phase],
            device_id={"sta": other_sta, "win": other_win}, device_id_type=MESH)

    def local_copy(src, dst, phase):
        return pltpu.make_async_copy(src, dst, recv_sem.at[phase])

    def wait_all(dst, phase):
        pltpu.make_async_copy(dst, dst, recv_sem.at[phase]).wait()
        part = dst.at[pl.ds(0, dst.shape[0] - 1)]
        pltpu.make_async_copy(part, part, send_sem.at[phase]).wait()

    def green_rows(comp, block, lo):
        rows = pl.ds(pl.multiple_of(block * LANES + lo, ROWS), ROWS)
        return (green[2 * comp, rows, :].astype(jnp.float32),
                green[2 * comp + 1, rows, :].astype(jnp.float32))

    def back_block(block, lo):
        rows = pl.ds(pl.multiple_of(block * LANES + lo, ROWS), ROWS)
        trace = u[rows, :] * weight
        re = im = None
        for comp in range(comps):
            gr, gi = green_rows(comp, block, lo)
            tr, ti = trace[:, 2 * comp:2 * comp + 1], trace[:, 2 * comp + 1:2 * comp + 2]
            a, b = gr * tr + gi * ti, gr * ti - gi * tr
            re, im = (a, b) if re is None else (re + a, im + b)
        return re, im

    def back_rows(lo):
        rows = pl.ds(lo, ROWS)
        for i in range(npair):
            ure, uim = back_block(npair + i, lo)
            lre, lim = back_block(npair - 1 - i, lo)
            qbuf[4 * i, rows, :] = ure + lre
            qbuf[4 * i + 1, rows, :] = uim + lim
            qbuf[4 * i + 2, rows, :] = ure - lre
            qbuf[4 * i + 3, rows, :] = uim - lim

    def project(norm2, turn):
        norm_row = jnp.broadcast_to(norm2, (1, LANES))

        def group(g, carry):
            for t in range(tiles):
                lanes = slice(t * LANES, (t + 1) * LANES)
                acc = [[None] * (2 * npair) for _ in range(group_rows)]
                for lb in range(LANES // 8):
                    rows = slice(lb * 8, lb * 8 + 8)
                    q = [qbuf[j, rows, lanes] for j in range(4 * npair)]
                    for j in range(group_rows):
                        c = cos_t[g * group_rows + j, rows, lanes]
                        s = sin_t[g * group_rows + j, rows, lanes]
                        for i in range(npair):
                            x = c * q[4 * i] - s * q[4 * i + 1]
                            y = c * q[4 * i + 3] + s * q[4 * i + 2]
                            if lb:
                                x, y = acc[j][2 * i] + x, acc[j][2 * i + 1] + y
                            acc[j][2 * i], acc[j][2 * i + 1] = x, y
                for j in range(group_rows):
                    w = g * group_rows + j
                    total = None
                    for i in range(npair):
                        part = (cd_row[2 * i, w, :, lanes] * acc[j][2 * i]
                                - cd_row[2 * i + 1, w, :, lanes] * acc[j][2 * i + 1])
                        total = part if total is None else total + part
                    row = jnp.sum(total, axis=0, keepdims=True)
                    send[g, j:j + 1, lanes] = row
                    if t == 0:
                        send[g, j:j + 1, width:] = norm_row
            phase = 1 + 3 * turn

            @pl.when(g != sta)
            def _():
                remote(send.at[g], recv.at[turn, sta], phase, g, win).start()

            @pl.when(g == sta)
            def _():
                local_copy(send.at[g], recv.at[turn, sta], phase).start()
            return carry
        lax.fori_loop(0, nsta, group, 0)

    def all_reduce(turn):
        phase = 1 + 3 * turn
        wait_all(recv.at[turn], phase)
        piece[...] = jnp.sum(recv[turn], axis=0)
        for b in near:
            if b:
                remote(piece, level.at[turn, win], phase + 1, sta, wins[b]).start()
        local_copy(piece, level.at[turn, win], phase + 1).start()
        wait_all(level.at[turn], phase + 1)
        summed = jnp.sum(level[turn], axis=0)
        total_piece[...] = summed[:, :width]
        for a in range(nsta - 1, 0, -1):
            remote(total_piece, full.at[turn, sta], phase + 2, stas[a], win).start()
        local_copy(total_piece, full.at[turn, sta], phase + 2).start()
        wait_all(full.at[turn], phase + 2)
        return summed[0:1, width:width + 1]

    def image(turn):
        for d in range(nsta):
            right[d * group_rows:(d + 1) * group_rows, :] = full[turn, d]
        return right[...]

    def square_sum(x):
        return jnp.sum(jnp.sum(x * x, axis=0, keepdims=True), axis=1, keepdims=True)

    tmp[:, 0:LANES] = jnp.zeros((LANES, LANES), jnp.float32)
    start = pl.multiple_of(lax.rem(sta, per_tile) * local_p, local_p)
    turned[...] = jnp.zeros_like(turned)
    onset_copy.wait()
    tmp[0:local_w, 0:local_p] = onset_own[...].astype(jnp.float32)
    turned[pl.ds(start, LANES), :] = tmp[:, 0:LANES].T
    onset[...] = turned[0:LANES, :].T[0:local_w, :]
    pl.semaphore_wait(barrier, ndev - 1)
    for other_sta, other_win in peers:
        remote(onset, on_recv.at[me], 0, other_sta, other_win).start()
    local_copy(onset, on_recv.at[me], 0).start()

    tmp[...] = jnp.zeros_like(tmp)
    rec_copy.wait()
    for comp in range(comps):
        for part in range(2):
            tmp[2 * comp + part:2 * comp + part + 1, 0:bins] = rec[0, comp, part:part + 1, :]
    for block in range(nblk):
        lanes = slice(block * LANES, (block + 1) * LANES)
        u[lanes, :] = tmp[:, lanes].T * weight
    first_norm = square_sum(u[...])
    green_copy.wait()
    for comp in range(comps):
        for part in range(2):
            for block in range(nblk):
                rows = slice(block * LANES, (block + 1) * LANES)
                for t in range(tiles):
                    lanes = slice(t * LANES, (t + 1) * LANES)
                    green[2 * comp + part, rows, lanes] = green_raw[0, comp, part, lanes, rows].T

    def first(step, carry):
        back_rows(pl.multiple_of(step * ROWS, ROWS))
        return carry
    lax.fori_loop(0, LANES // ROWS, first, 0)

    wait_all(on_recv, 0)
    for z in range(nwin):
        for t in range(tiles):
            block = on_recv[(t * per_tile) * nwin + z]
            for s in range(1, per_tile):
                block = block + on_recv[(t * per_tile + s) * nwin + z]
            on_all[z * local_w:(z + 1) * local_w, t * LANES:(t + 1) * LANES] = block.astype(jnp.int32)
    for i in range(npair):
        c, s = cos_sin(on_all[...] * (LANES // 2 + i * LANES))
        cd[2 * i], cd[2 * i + 1] = c, s
        for w in range(windows):
            cd_row[2 * i, w], cd_row[2 * i + 1, w] = c[w:w + 1], s[w:w + 1]
    for w in range(windows):
        on_row[w] = on_all[w:w + 1, :]
    centre = win * bins + (bins - LANES) // 2

    def tables(w, carry):
        rowv = on_row[w]
        low = lax.broadcasted_iota(jnp.int32, (ROWS, patches), 0) + centre
        c0, s0 = cos_sin(low * rowv)
        high = lax.broadcasted_iota(jnp.int32, (LANES // ROWS, patches), 0) * ROWS
        c1, s1 = cos_sin(high * rowv)
        cos_t[w, 0:ROWS, :] = c0
        sin_t[w, 0:ROWS, :] = s0
        for lb in range(1, LANES // ROWS):
            ch, sh = c1[lb:lb + 1], s1[lb:lb + 1]
            cos_t[w, lb * ROWS:(lb + 1) * ROWS, :] = c0 * ch - s0 * sh
            sin_t[w, lb * ROWS:(lb + 1) * ROWS, :] = s0 * ch + c0 * sh
        return carry
    lax.fori_loop(0, windows, tables, 0)

    project(first_norm, 0)
    norm2 = all_reduce(0)
    beta = jnp.sqrt(norm2)
    v = image(0) / beta
    alpha = jnp.sqrt(square_sum(v))
    v = v / alpha
    search = v
    estimate = jnp.zeros_like(v)
    phi_bar, rho_bar = beta, alpha

    for sweep in range(ITERS):
        for i in range(npair):
            coef[2 * i] = v * cd[2 * i]
            coef[2 * i + 1] = v * cd[2 * i + 1]
        right[...] = v

        def forward(step, carry, alpha=alpha, beta=beta):
            lo = pl.multiple_of(step * ROWS, ROWS)
            spectra = [[] for _ in range(2 * nblk)]
            for t in range(tiles):
                lanes = slice(t * LANES, (t + 1) * LANES)
                acc = None
                for w in range(windows):
                    c = cos_t[w, pl.ds(lo, ROWS), lanes]
                    s = sin_t[w, pl.ds(lo, ROWS), lanes]
                    terms = []
                    for i in range(2 * npair):
                        a = coef[i, w:w + 1, lanes]
                        terms += [a * c, a * s]
                    acc = terms if acc is None else [x + y for x, y in zip(acc, terms)]
                for i in range(npair):
                    x1, x2, y1, y2 = acc[4 * i:4 * i + 4]
                    up, low = npair + i, npair - 1 - i
                    spectra[2 * up].append(x1 - y2)
                    spectra[2 * up + 1].append(-x2 - y1)
                    spectra[2 * low].append(x1 + y2)
                    spectra[2 * low + 1].append(y1 - x2)
            lane = lax.broadcasted_iota(jnp.int32, (ROWS, LANES), 1)
            for block in range(nblk):
                sre, sim = [[x.astype(jnp.bfloat16).astype(jnp.float32) for x in spectra[2 * block + k]] for k in range(2)]
                data = jnp.zeros((ROWS, LANES), jnp.float32)
                for comp in range(comps):
                    gr, gi = green_rows(comp, block, lo)
                    re = im = 0.0
                    for t in range(tiles):
                        lanes = slice(t * LANES, (t + 1) * LANES)
                        re = re + (gr[:, lanes] * sre[t] - gi[:, lanes] * sim[t])
                        im = im + (gr[:, lanes] * sim[t] + gi[:, lanes] * sre[t])
                    data = jnp.where(lane == 2 * comp, jnp.sum(re, axis=1, keepdims=True), data)
                    data = jnp.where(lane == 2 * comp + 1, jnp.sum(im, axis=1, keepdims=True), data)
                rows = pl.ds(pl.multiple_of(block * LANES + lo, ROWS), ROWS)
                u[rows, :] = data * weight - (alpha / beta) * u[rows, :]
            back_rows(lo)
            return carry
        lax.fori_loop(0, LANES // ROWS, forward, 0)

        project(square_sum(u[...]), 1 + sweep)
        norm2 = all_reduce(1 + sweep)
        old = right[...]
        beta = jnp.sqrt(norm2)
        v = image(1 + sweep) / beta - beta * old
        alpha = jnp.sqrt(square_sum(v))
        v = v / alpha
        rho = jnp.sqrt(rho_bar * rho_bar + beta * beta)
        cosine_rot = rho_bar / rho
        sine_rot = beta / rho
        theta = sine_rot * alpha
        rho_bar = -cosine_rot * alpha
        phi = cosine_rot * phi_bar
        phi_bar = sine_rot * phi_bar
        estimate = estimate + phi / rho * search
        search = v - theta / rho * search
    tmp[...] = jnp.zeros_like(tmp)
    for value, out in ((estimate, est_out), (search * math.sqrt(patches * windows), dir_out)):
        tmp[0:windows, 0:patches] = value
        for t in range(tiles):
            lanes = slice(t * LANES, (t + 1) * LANES)
            turned[lanes, :] = tmp[:, lanes].T
        rows = turned[pl.ds(pl.multiple_of(sta * local_p, local_p), LANES), :].T
        own = rows[0:local_w, 0:local_p]
        for z in range(1, nwin):
            own = jnp.where(win == z, rows[z * local_w:(z + 1) * local_w, 0:local_p], own)
        out[...] = own
    scale = phi_bar / beta
    for block in range(nblk):
        lanes = slice(block * LANES, (block + 1) * LANES)
        flipped = (u[lanes, :] * scale).T
        for comp in range(comps):
            mis_out[0, comp, :, lanes] = flipped[2 * comp:2 * comp + 2, :]


def local(nsta, nwin, green, records, onsets, mask):
    local_p, local_w = onsets.shape
    comps = green.shape[1]
    patches, windows = local_p * nsta, local_w * nwin
    bins = green.shape[4]
    ndev = nsta * nwin
    width = patches
    group_rows = windows // nsta
    npair = bins // LANES // 2
    cfg = (nsta, nwin, patches, windows, bins, comps, local_w, local_p)
    f32 = jnp.float32
    turns = ITERS + 1
    slip, direction, misfit = pl.pallas_call(
        functools.partial(kernel, cfg),
        out_shape=(jax.ShapeDtypeStruct((local_w, local_p), f32),
                   jax.ShapeDtypeStruct((local_w, local_p), f32),
                   jax.ShapeDtypeStruct((1, comps, 2, bins), f32)),
        in_specs=[pl.BlockSpec(memory_space=pl.ANY),
                  pl.BlockSpec(memory_space=pl.ANY),
                  pl.BlockSpec(memory_space=pl.ANY),
                  pl.BlockSpec(memory_space=pltpu.SMEM)],
        out_specs=(pl.BlockSpec(memory_space=pltpu.VMEM),) * 3,
        scratch_shapes=[
            pltpu.VMEM((1, comps, 2, patches, bins), jnp.bfloat16),
            pltpu.VMEM((2 * comps, bins, patches), jnp.bfloat16),
            pltpu.SemaphoreType.DMA,
            pltpu.VMEM((1, comps, 2, bins), f32),
            pltpu.SemaphoreType.DMA,
            pltpu.VMEM((local_w, local_p), jnp.int32),
            pltpu.SemaphoreType.DMA,
            pltpu.VMEM((LANES, max(bins, patches)), f32),
            pltpu.VMEM((local_w, LANES), f32),
            pltpu.VMEM((ndev, local_w, LANES), f32),
            pltpu.VMEM((windows, patches), jnp.int32),
            pltpu.VMEM((windows, 1, patches), jnp.int32),
            pltpu.VMEM((windows, LANES, patches), f32),
            pltpu.VMEM((windows, LANES, patches), f32),
            pltpu.VMEM((2 * npair, windows, patches), f32),
            pltpu.VMEM((2 * npair, windows, 1, patches), f32),
            pltpu.VMEM((2 * npair, windows, patches), f32),
            pltpu.VMEM((4 * npair, LANES, patches), f32),
            pltpu.VMEM((bins, LANES), f32),
            pltpu.VMEM((windows, patches), f32),
            pltpu.VMEM((patches + LANES, LANES), f32),
            pltpu.VMEM((nsta, group_rows, width + LANES), f32),
            pltpu.VMEM((turns, nsta, group_rows, width + LANES), f32),
            pltpu.VMEM((group_rows, width + LANES), f32),
            pltpu.VMEM((turns, nwin, group_rows, width + LANES), f32),
            pltpu.VMEM((group_rows, width), f32),
            pltpu.VMEM((turns, nsta, group_rows, width), f32),
            pltpu.SemaphoreType.DMA((1 + 3 * turns,)),
            pltpu.SemaphoreType.DMA((1 + 3 * turns,)),
        ],
        compiler_params=pltpu.CompilerParams(
            collective_id=0, has_side_effects=True, vmem_limit_bytes=56 * 2**20),
    )(green, records, onsets.T, mask)
    return slip.T, direction.T, misfit


def solution(mesh):
    return jax.shard_map(
        functools.partial(local, mesh.shape["sta"], mesh.shape["win"]),
        mesh=mesh,
        in_specs=(
            P("sta", None, None, None, "win"),
            P("sta", None, None, "win"),
            P("sta", "win"),
            P("sta", None),
        ),
        out_specs=(P("sta", "win"), P("sta", "win"), P("sta", None, None, "win")),
        check_vma=False,
    )
```
